32 devices in a mesh: dp: 16 (over z, y, x), fsdp: 2 (over core).
Axes of the slice: x: 2, y: 2, z: 4, core: 2. Of those that a mesh axis runs over, the one named last changes fastest.
Arguments:
- hidden_in: bfloat16 [32, 1024, 768], P(('dp', 'fsdp')), may hold values from -6 to 6
- row_grad: bfloat16 [32, 1024, 768], P(('dp', 'fsdp')), may hold values from -6 to 6
- segment_ids: int32 [32, 1024], P(('dp', 'fsdp')), may hold values from 0 to 15, as said below
- query_cls: int32 [32, 8], P(('dp', 'fsdp')), may hold values from 0 to 1022, as said below
- passage_cls: int32 [32, 8], P(('dp', 'fsdp')), may hold values from 16 to 1023, as said below
- positives: int32 [256], replicated, may hold values from 0 to 255
- w_query: float32 [768, 768], P(('dp', 'fsdp')), may hold values from -0.3125 to 0.3125
- w_key: float32 [768, 768], P(('dp', 'fsdp')), may hold values from -0.21875 to 0.21875
- w_value: float32 [768, 768], P(('dp', 'fsdp')), may hold values from -0.21875 to 0.21875
- w_output: float32 [768, 768], P(('dp', 'fsdp')), may hold values from -0.625 to 0.625
- b_query: float32 [768], P(('dp', 'fsdp')), may hold values from -3 to 3
- b_value: float32 [768], P(('dp', 'fsdp')), may hold values from -3 to 3
- b_output: float32 [768], P(('dp', 'fsdp')), may hold values from -3 to 3
- attn_gain: float32 [768], P(('dp', 'fsdp')), may hold values from 0.5 to 1.5
- attn_shift: float32 [768], P(('dp', 'fsdp')), may hold values from -2 to 2
- w_inner: float32 [768, 3072], P(('dp', 'fsdp')), may hold values from -0.21875 to 0.21875
- b_inner: float32 [3072], P(('dp', 'fsdp')), may hold values from -3 to 3
- w_outer: float32 [3072, 768], P(('dp', 'fsdp')), may hold values from -0.109375 to 0.109375
- b_outer: float32 [768], P(('dp', 'fsdp')), may hold values from -2 to 2
- ffn_gain: float32 [768], P(('dp', 'fsdp')), may hold values from 0.5 to 1.5
- ffn_shift: float32 [768], P(('dp', 'fsdp')), may hold values from -2 to 2
Outputs:
- query_loss: float32 [256], P(('dp', 'fsdp'))
- hidden_out: bfloat16 [32, 1024, 768], P(('dp', 'fsdp'))
- hidden_grad: float32 [32, 1024, 768], P(('dp', 'fsdp'))
- w_query_grad: float32 [768, 768], P(('dp', 'fsdp'))
- w_key_grad: float32 [768, 768], P(('dp', 'fsdp'))
- w_value_grad: float32 [768, 768], P(('dp', 'fsdp'))
- w_output_grad: float32 [768, 768], P(('dp', 'fsdp'))
- b_query_grad: float32 [768], P(('dp', 'fsdp'))
- b_value_grad: float32 [768], P(('dp', 'fsdp'))
- b_output_grad: float32 [768], P(('dp', 'fsdp'))
- attn_gain_grad: float32 [768], P(('dp', 'fsdp'))
- attn_shift_grad: float32 [768], P(('dp', 'fsdp'))
- w_inner_grad: float32 [768, 3072], P(('dp', 'fsdp'))
- b_inner_grad: float32 [3072], P(('dp', 'fsdp'))
- w_outer_grad: float32 [3072, 768], P(('dp', 'fsdp'))
- b_outer_grad: float32 [768], P(('dp', 'fsdp'))
- ffn_gain_grad: float32 [768], P(('dp', 'fsdp'))
- ffn_shift_grad: float32 [768], P(('dp', 'fsdp'))
The draws below stay inside these ranges and needn't reach their ends.
Inputs may be any that keep to these rules, and one draw needn't show every extreme that they name: `segment_ids`: each row holds 16 segments numbered in order of position, a query segment (even number) and a passage segment (odd number) alternating. `query_cls`: the first position of each query segment of the row, in order. `passage_cls`: the first position of each passage segment of the row, in order.
All inputs are finite; a program needn't handle non-finite values.
Results may differ from the reference program's by a relative error of at most 0.013.
The reference program's roundings to bfloat16 on the way count: a program that leaves them out, or rounds other values in their place, can miss the bound.
Values may be sent and summed in bfloat16 or wider, within the bound.
No kernel may reach another device: no remote copies, remote signals or barrier semaphores. Data moves between devices by JAX's collectives and lax.ppermute only.
A program may use at most 256 MiB of HBM per device.

```python
import math
import jax
import jax.numpy as jnp
from jax import lax

D = 768
HEADS = 12
HEAD = 64
FF = 3072
SEQ = 1024
PAIRS = 8
ROWS = 32
QUERIES = 256
PASSAGES = 256


def row_layout(key):
    key_query, key_share = jax.random.split(key)
    query_len = jax.random.randint(key_query, (PAIRS,), SEQ // 64, SEQ // 32 + 1).astype(jnp.int32)
    remain = SEQ - jnp.sum(query_len)
    shares = jax.random.randint(key_share, (PAIRS,), 50, 100).astype(jnp.int32)
    passage_len = remain * shares // jnp.sum(shares)
    passage_len = passage_len.at[PAIRS - 1].add(remain - jnp.sum(passage_len))
    lengths = jnp.stack([query_len, passage_len], axis=1).reshape(2 * PAIRS)
    starts = jnp.cumsum(lengths) - lengths
    position = jnp.arange(SEQ, dtype=jnp.int32)
    segment = jnp.sum((position[:, None] >= starts[None, :]).astype(jnp.int32), axis=1) - 1
    return (segment.astype(jnp.int32), starts[0::2].astype(jnp.int32), starts[1::2].astype(jnp.int32))


def layout(key):
    return jax.vmap(row_layout)(jax.random.split(jax.random.fold_in(key, 7), ROWS))


def draw_segment_ids(key, part):
    return layout(key)[0]


def draw_query_cls(key, part):
    return layout(key)[1]


def draw_passage_cls(key, part):
    return layout(key)[2]


def plant(result, key, smallest, high):
    shape = result.shape
    index_at = [jax.random.randint(jax.random.fold_in(key, axis), (), 0, shape[axis]) for axis in range(len(shape))]
    result = result.at[tuple(index_at)].set(smallest)
    longest = shape.index(max(shape))
    index_at[longest] = (index_at[longest] + 1) % shape[longest]
    return result.at[tuple(index_at)].set(high)


def block_levels(stream_key, shape, shards, smallest, top_value):
    level, own = 1.0, jax.random.fold_in(stream_key, 6)
    for dim, parts in shards:
        draws = jnp.exp(jax.random.uniform(jax.random.fold_in(own, dim), (parts,), jnp.float32, smallest / len(shards), top_value / len(shards)))
        level = level * jnp.repeat(draws, shape[dim] // parts).reshape([-1 if axis == dim else 1 for axis in range(len(shape))])
    return level


def scatter_about(own_key, extent, width, most, cuts=(), kind=jnp.bfloat16):
    drawn = jax.random.normal(own_key, extent, jnp.float32) * width
    if len(cuts) > 0:
        drawn = block_levels(own_key, extent, cuts, -0.22, 0.18) * drawn
    return jnp.clip(drawn, min=-most, max=most).astype(kind)


def setup_inputs(seed: int = 0) -> dict:
    seeds = jax.random.split(jax.random.key(seed), 22)
    hidden_in = scatter_about(seeds[0], (ROWS, SEQ, D), 1.0, 6.0, ((0, 32),))
    row_grad = scatter_about(seeds[1], (ROWS, SEQ, D), 1.0, 6.0, ((0, 32),))
    segment_ids = draw_segment_ids(jax.random.fold_in(seeds[21], 71), 0)
    query_cls = draw_query_cls(jax.random.fold_in(seeds[21], 71), 0)
    passage_cls = draw_passage_cls(jax.random.fold_in(seeds[21], 71), 0)
    positives = plant(jax.random.randint(seeds[5], (QUERIES,), 0, PASSAGES), jax.random.fold_in(seeds[5], 1), 0, PASSAGES - 1).astype(jnp.int32)
    w_query = scatter_about(seeds[6], (D, D), (D // 2) ** -0.5, 0.3125, ((0, 32),), jnp.float32)
    w_key = scatter_about(seeds[7], (D, D), D ** -0.5, 0.21875, ((0, 32),), jnp.float32)
    w_value = scatter_about(seeds[8], (D, D), D ** -0.5, 0.21875, ((0, 32),), jnp.float32)
    w_output = scatter_about(seeds[9], (D, D), (D // 8) ** -0.5, 0.625, ((0, 32),), jnp.float32)
    b_query = scatter_about(seeds[10], (D,), 0.5, 3.0, ((0, 32),), jnp.float32)
    b_value = scatter_about(seeds[11], (D,), 0.5, 3.0, ((0, 32),), jnp.float32)
    b_output = scatter_about(seeds[12], (D,), 0.5, 3.0, ((0, 32),), jnp.float32)
    attn_gain = jnp.clip(1.0 + 0.1 * jax.random.normal(seeds[13], (D,), jnp.float32), 0.5, 1.5)
    attn_shift = scatter_about(seeds[14], (D,), 0.3, 2.0, ((0, 32),), jnp.float32)
    w_inner = scatter_about(seeds[15], (D, FF), D ** -0.5, 0.21875, ((0, 32),), jnp.float32)
    b_inner = scatter_about(seeds[16], (FF,), 0.5, 3.0, ((0, 32),), jnp.float32)
    w_outer = scatter_about(seeds[17], (FF, D), FF ** -0.5, 0.109375, ((0, 32),), jnp.float32)
    b_outer = scatter_about(seeds[18], (D,), 0.3, 2.0, ((0, 32),), jnp.float32)
    ffn_gain = jnp.clip(1.0 + 0.1 * jax.random.normal(seeds[19], (D,), jnp.float32), 0.5, 1.5)
    ffn_shift = scatter_about(seeds[20], (D,), 0.3, 2.0, ((0, 32),), jnp.float32)
    return {"hidden_in": hidden_in, "row_grad": row_grad, "segment_ids": segment_ids, "query_cls": query_cls, "passage_cls": passage_cls, "positives": positives, "w_query": w_query, "w_key": w_key, "w_value": w_value, "w_output": w_output, "b_query": b_query, "b_value": b_value, "b_output": b_output, "attn_gain": attn_gain, "attn_shift": attn_shift, "w_inner": w_inner, "b_inner": b_inner, "w_outer": w_outer, "b_outer": b_outer, "ffn_gain": ffn_gain, "ffn_shift": ffn_shift}


EPS = 1e-12
NEG = -1e+30
HIGH = lax.Precision.HIGHEST

@jax.custom_vjp
def low(v):
    return lax.optimization_barrier(v.astype(jnp.bfloat16)).astype(jnp.float32)

@jax.custom_vjp
def low_back(v):
    return v

def low_keep(v):
    return (low(v), None)

def low_pass(kept, grad):
    return (grad,)

def back_keep(v):
    return (v, None)

def back_low(kept, grad):
    return (low(grad),)
low.defvjp(low_keep, low_pass)
low_back.defvjp(back_keep, back_low)

def matmul(left, right):
    return jnp.dot(left, right, precision=HIGH, preferred_element_type=jnp.float32)

def both_low(value):
    return low_back(low(value))

def layer_norm(value, gain, shift):
    mean = lax.optimization_barrier(jnp.mean(value, axis=-1, keepdims=True))
    centred = value - mean
    spread = lax.optimization_barrier(jnp.mean(centred * centred, axis=-1, keepdims=True))
    return centred * lax.rsqrt(spread + EPS) * gain + shift

def row_block(params, inputs, segment):
    w_query, w_key, w_value, w_output, b_query, b_value, b_output, attn_gain, attn_shift, w_inner, b_inner, w_outer, b_outer, ffn_gain, ffn_shift = params
    queries = both_low(matmul(inputs, w_query) + b_query).reshape(SEQ, HEADS, HEAD)
    keys_all = both_low(matmul(inputs, w_key)).reshape(SEQ, HEADS, HEAD)
    values = both_low(matmul(inputs, w_value) + b_value).reshape(SEQ, HEADS, HEAD)
    raw_scores = jnp.einsum('qhd,khd->hqk', queries, keys_all, precision=HIGH, preferred_element_type=jnp.float32)
    scores = low_back(raw_scores * HEAD ** (-0.5))
    same = segment[:, None] == segment[None, :]
    scores = jnp.where(same[None], scores, NEG)
    probs = jax.nn.softmax(scores, axis=-1)
    context = jnp.einsum('hqk,khd->qhd', low(probs), values, precision=HIGH, preferred_element_type=jnp.float32)
    context = both_low(context.reshape(SEQ, D))
    branch = low_back(matmul(context, w_output) + b_output)
    middle = layer_norm(inputs + branch, attn_gain, attn_shift)
    pre_act = low_back(matmul(low(middle), w_inner) + b_inner)
    activated = low(jax.nn.gelu(pre_act, approximate=False))
    update = low_back(matmul(activated, w_outer) + b_outer)
    return layer_norm(middle + update, ffn_gain, ffn_shift)

def reference(hidden_in, row_grad, segment_ids, query_cls, passage_cls, positives, w_query, w_key, w_value, w_output, b_query, b_value, b_output, attn_gain, attn_shift, w_inner, b_inner, w_outer, b_outer, ffn_gain, ffn_shift):
    params = (w_query, w_key, w_value, w_output, b_query, b_value, b_output, attn_gain, attn_shift, w_inner, b_inner, w_outer, b_outer, ffn_gain, ffn_shift)
    inputs = hidden_in.astype(jnp.float32)
    cotangent = row_grad.astype(jnp.float32)
    score_scale = 4.0 / math.sqrt(D)
    row_base = (jnp.arange(ROWS, dtype=jnp.int32) * SEQ)[:, None]
    query_index = (query_cls + row_base).reshape(QUERIES).astype(jnp.int32)
    passage_index = (passage_cls + row_base).reshape(PASSAGES).astype(jnp.int32)
    column_ids = jnp.arange(PASSAGES, dtype=jnp.int32)
    hit = (column_ids[None, :] == positives[:, None]).astype(jnp.float32)

    def objective(rows_in, masters):
        rounded = tuple((low(item) for item in masters))

        def one_row(pair):
            return row_block(rounded, pair[0], pair[1])
        output = lax.map(jax.checkpoint(one_row), (rows_in, segment_ids))
        flat = output.reshape(ROWS * SEQ, D)
        query_emb = low(flat[query_index])
        passage_emb = low(flat[passage_index])
        raw = matmul(query_emb, passage_emb.T)
        scores = score_scale * low_back(raw)
        losses = jax.nn.logsumexp(scores, axis=-1) - lax.optimization_barrier(jnp.sum(hit * scores, axis=-1))
        total = jnp.sum(losses) + jnp.sum(output * cotangent)
        return (total, (losses, output))
    total, pullback, extras = jax.vjp(objective, inputs, params, has_aux=True)
    losses, output = extras
    input_grad, param_grads = pullback(jnp.ones_like(total))
    return (losses, output.astype(jnp.bfloat16), input_grad) + tuple(param_grads)
```

```python
import math

import jax
import jax.numpy as jnp
from jax import lax
from jax.experimental import pallas as pl
from jax.experimental.pallas import tpu as pltpu
from jax.sharding import PartitionSpec as P

HEADS = 12
HEAD = 64
EPS = 1e-12
NEG = -1e30
QB = 128
WINDOWS = (256, 384, 512)
AXES = ("dp", "fsdp")
F32 = jnp.float32
BF16 = jnp.bfloat16


def _bounds(starts_ref, first, last, length):
    low = jnp.int32(0)
    high = jnp.int32(length)
    for s in range(starts_ref.shape[0]):
        at = starts_ref[s]
        low = jnp.maximum(low, jnp.where(at <= first, at, 0))
        high = jnp.minimum(high, jnp.where(at > last, at, length))
    return low, high

def _row_bounds(starts_ref, pos, length):
    low = jnp.zeros_like(pos)
    high = jnp.full_like(pos, length)
    for s in range(starts_ref.shape[0]):
        at = starts_ref[s]
        low = jnp.maximum(low, jnp.where(pos >= at, at, 0))
        high = jnp.minimum(high, jnp.where(pos < at, at, length))
    return low, high

def _variants(starts_ref, length, body):
    first = pl.program_id(0) * QB
    low, high = _bounds(starts_ref, first, first + QB - 1, length)
    base = (low // 16) * 16
    need = high - base
    done = jnp.bool_(False)
    sizes = [w for w in WINDOWS if w < length] + [length]
    prev = 0
    for w in sizes:
        @pl.when(jnp.logical_and(need > prev, need <= w))
        def _(w=w):
            start = pl.multiple_of(jnp.minimum(base, length - w), 16)
            body(w, start, first)
        prev = w

def _pair(block):
    lane = lax.broadcasted_iota(jnp.int32, block.shape, 1)
    zero = jnp.zeros_like(block)
    return jnp.concatenate([jnp.where(lane < HEAD, block, zero), jnp.where(lane < HEAD, zero, block)], axis=0)

def _pick(both):
    half = both.shape[0] // 2
    lane = lax.broadcasted_iota(jnp.int32, (half, both.shape[1]), 1)
    return jnp.where(lane < HEAD, both[:half], both[half:])

def fwd_kernel(starts_ref, q_ref, k_ref, v_ref, c_ref, lse_ref):
    length = k_ref.shape[0]
    def body(w, start, first):
        pos = first + lax.broadcasted_iota(jnp.int32, (QB, 1), 0)
        low, high = _row_bounds(starts_ref, pos, length)
        key = start + lax.broadcasted_iota(jnp.int32, (QB, w), 1)
        bias = jnp.where(jnp.logical_and(key >= low, key < high), 0.0, NEG)
        lane = lax.broadcasted_iota(jnp.int32, (QB, 128), 1)
        lse = jnp.zeros((QB, 128), jnp.float32)
        for h in range(HEADS // 2):
            cols = slice(h * 128, h * 128 + 128)
            q2 = _pair(q_ref[:, cols] * jnp.bfloat16(HEAD ** -0.5))
            kw = k_ref[pl.ds(start, w), cols]
            s = lax.dot_general(q2, kw, (((1,), (1,)), ((), ())), preferred_element_type=jnp.float32)
            s = s + jnp.concatenate([bias, bias], axis=0)
            m = jnp.max(s, axis=-1, keepdims=True)
            e = jnp.exp(s - m)
            l = jnp.sum(e, axis=-1, keepdims=True)
            p = (e * (1.0 / l)).astype(jnp.bfloat16)
            o = jnp.dot(p, v_ref[pl.ds(start, w), cols], preferred_element_type=jnp.float32)
            c_ref[:, cols] = _pick(o).astype(jnp.bfloat16)
            t = m + jnp.log(l)
            lse = jnp.where(lane == 2 * h, t[:QB], lse)
            lse = jnp.where(lane == 2 * h + 1, t[QB:], lse)
        lse_ref[...] = jnp.transpose(lse)[:16]
    _variants(starts_ref, length, body)

def attn_fwd(starts, qkv):
    length = qkv.shape[0]; width = HEADS * HEAD
    return pl.pallas_call(
        fwd_kernel,
        out_shape=(jax.ShapeDtypeStruct((length, width), jnp.bfloat16), jax.ShapeDtypeStruct((16, length), jnp.float32)),
        grid_spec=pltpu.PrefetchScalarGridSpec(
            num_scalar_prefetch=1, grid=(length // QB,),
            in_specs=[pl.BlockSpec((QB, width), lambda i, s: (i, 0)),
                      pl.BlockSpec((length, width), lambda i, s: (0, 1)),
                      pl.BlockSpec((length, width), lambda i, s: (0, 2))],
            out_specs=[pl.BlockSpec((QB, width), lambda i, s: (i, 0)), pl.BlockSpec((16, QB), lambda i, s: (0, i))]),
        compiler_params=pltpu.CompilerParams(dimension_semantics=("arbitrary",), vmem_limit_bytes=48 << 20),
        name="attend",
    )(starts, qkv, qkv, qkv)

def bwd_kernel(starts_ref, q_ref, k_ref, v_ref, dc_ref, lse_ref, out_ref, dk_ref, dv_ref):
    length = k_ref.shape[0]; width = HEADS * HEAD
    step = pl.program_id(0)
    @pl.when(step == 0)
    def _():
        dk_ref[...] = jnp.zeros_like(dk_ref)
        dv_ref[...] = jnp.zeros_like(dv_ref)
    def body(w, start, first):
        pos = first + lax.broadcasted_iota(jnp.int32, (1, QB), 1)
        low, high = _row_bounds(starts_ref, pos, length)
        key = start + lax.broadcasted_iota(jnp.int32, (w, QB), 0)
        bias = jnp.where(jnp.logical_and(key >= low, key < high), 0.0, NEG)
        row = lax.broadcasted_iota(jnp.int32, (128, QB), 0)
        for h in range(HEADS // 2):
            cols = slice(h * 128, h * 128 + 128)
            q2 = _pair(q_ref[:, cols] * jnp.bfloat16(HEAD ** -0.5))
            d2 = _pair(dc_ref[:, cols])
            kw = k_ref[pl.ds(start, w), cols]
            vw = v_ref[pl.ds(start, w), cols]
            s = lax.dot_general(kw, q2, (((1,), (1,)), ((), ())), preferred_element_type=jnp.float32)
            lse = jnp.concatenate([lse_ref[2 * h:2 * h + 1, :], lse_ref[2 * h + 1:2 * h + 2, :]], axis=1)
            p = jnp.exp(s + jnp.concatenate([bias, bias], axis=1) - lse)
            dp = lax.dot_general(vw, d2, (((1,), (1,)), ((), ())), preferred_element_type=jnp.float32)
            delta = jnp.sum(p * dp, axis=0, keepdims=True)
            ds = (p * (dp - delta)).astype(jnp.bfloat16)
            dv_ref[pl.ds(start, w), cols] += jnp.dot(p.astype(jnp.bfloat16), d2, preferred_element_type=jnp.float32)
            dk_ref[pl.ds(start, w), cols] += jnp.dot(ds, q2, preferred_element_type=jnp.float32)
            dqt = lax.dot_general(kw, ds, (((0,), (0,)), ((), ())), preferred_element_type=jnp.float32)
            dqt = jnp.where(row < HEAD, dqt[:, :QB], dqt[:, QB:]) * HEAD ** -0.5
            out_ref[pl.ds(pl.multiple_of(first, QB), QB), cols] = jnp.transpose(dqt).astype(jnp.bfloat16)
    _variants(starts_ref, length, body)
    @pl.when(step == pl.num_programs(0) - 1)
    def _():
        out_ref[:, width:2 * width] = dk_ref[...].astype(jnp.bfloat16)
        out_ref[:, 2 * width:] = dv_ref[...].astype(jnp.bfloat16)

def attn_bwd(starts, qkv, dc, lse):
    length = qkv.shape[0]; width = HEADS * HEAD
    return pl.pallas_call(
        bwd_kernel,
        out_shape=jax.ShapeDtypeStruct((length, 3 * width), jnp.bfloat16),
        grid_spec=pltpu.PrefetchScalarGridSpec(
            num_scalar_prefetch=1, grid=(length // QB,),
            in_specs=[pl.BlockSpec((QB, width), lambda i, s: (i, 0)),
                      pl.BlockSpec((length, width), lambda i, s: (0, 1)),
                      pl.BlockSpec((length, width), lambda i, s: (0, 2)),
                      pl.BlockSpec((QB, width), lambda i, s: (i, 0)),
                      pl.BlockSpec((16, QB), lambda i, s: (0, i))],
            out_specs=pl.BlockSpec((length, 3 * width), lambda i, s: (0, 0)),
            scratch_shapes=[pltpu.VMEM((length, width), jnp.float32), pltpu.VMEM((length, width), jnp.float32)]),
        compiler_params=pltpu.CompilerParams(dimension_semantics=("arbitrary",), vmem_limit_bytes=56 << 20),
        name="attend_back",
    )(starts, qkv, qkv, qkv, dc, lse)


def matmul(left, right):
    return jnp.dot(left, right, preferred_element_type=F32)


def contract_rows(left, right):
    return lax.dot_general(left, right, (((0,), (0,)), ((), ())), preferred_element_type=F32)


def contract_cols(left, right):
    return lax.dot_general(left, right, (((1,), (1,)), ((), ())), preferred_element_type=F32)


def norm_forward(value, gain, shift):
    mean = jnp.mean(value, axis=-1, keepdims=True)
    centred = value - mean
    spread = jnp.mean(centred * centred, axis=-1, keepdims=True)
    scaling = lax.rsqrt(spread + EPS)
    normed = centred * scaling
    return (normed * gain + shift, normed, scaling)


def norm_backward(grad, normed, scaling, gain):
    scaled = grad * gain
    first_mean = jnp.mean(scaled, axis=-1, keepdims=True)
    second_mean = jnp.mean(scaled * normed, axis=-1, keepdims=True)
    result = scaling * (scaled - first_mean - normed * second_mean)
    return (result, jnp.sum(grad * normed, axis=0), jnp.sum(grad, axis=0))


def gelu_parts(pre_act):
    cdf_part = 0.5 * (1.0 + lax.erf(pre_act * (1.0 / math.sqrt(2.0))))
    slope = cdf_part + pre_act * jnp.exp(-0.5 * pre_act * pre_act) * (1.0 / math.sqrt(2.0 * math.pi))
    return (pre_act * cdf_part, slope)


class Cube:
    def __init__(self, chips):
        bits = chips.bit_length() - 1
        side = bits // 3
        self.n = 2 * chips
        self.total = bits + 1
        x_bits = list(range(1, 1 + side))
        y_bits = list(range(1 + side, 1 + 2 * side))
        z_bits = list(range(1 + 2 * side, 1 + bits))
        far = list(reversed(z_bits))
        self.order = [(b, b) for b in far]
        self.order += list(zip(x_bits, y_bits)) + list(zip(y_bits, x_bits))
        self.me = lax.axis_index(AXES)
        self.core = self.me & 1

    def bit(self, pair):
        return (self.me >> jnp.where(self.core == 0, pair[0], pair[1])) & 1

    def swap(self, value, pair):
        perm = [(i, i ^ (1 << pair[i & 1])) for i in range(self.n)]
        return lax.ppermute(value, AXES, perm)

    def gather(self, shard):
        have = shard
        for pair in self.order:
            other = self.swap(have, pair)
            mine_low = self.bit(pair) == 0
            have = jnp.stack([jnp.where(mine_low, have, other), jnp.where(mine_low, other, have)])
        other = self.swap(have, (0, 0))
        mine_low = self.core == 0
        count = len(self.order)
        sides = []
        for side, whole in enumerate((jnp.where(mine_low, have, other), jnp.where(mine_low, other, have))):
            place = {pair[side]: count - 1 - at for at, pair in enumerate(self.order)}
            axes = [place[b] for b in range(self.total - 1, 0, -1)]
            sides.append(jnp.transpose(whole, axes + list(range(count, whole.ndim))))
        whole = jnp.stack(sides, axis=count)
        return whole.reshape((self.n * shard.shape[0],) + shard.shape[1:])

    def scatter(self, grad):
        rows = grad.shape[0] // self.n
        have = grad.reshape((2,) * self.total + (rows,) + grad.shape[1:])
        names = [list(range(self.total - 1, -1, -1))] * 2
        for pair in [(0, 0)] + self.order[::-1]:
            bit = self.bit(pair)
            kept, sent, left = [], [], []
            for side in range(2):
                axis = names[side].index(pair[side])
                kept.append(lax.dynamic_index_in_dim(have, bit, axis, keepdims=False))
                sent.append(lax.dynamic_index_in_dim(have, 1 - bit, axis, keepdims=False))
                left.append(names[side][:axis] + names[side][axis + 1:])
            names = left
            if pair[0] == pair[1] and names[0] == names[1]:
                keep, send = kept[0], sent[0]
            else:
                keep = jnp.where(self.core == 0, kept[0], kept[1])
                send = jnp.where(self.core == 0, sent[0], sent[1])
            have = keep.astype(F32) + self.swap(send.astype(BF16), pair).astype(F32)
        return have


def as_columns(vectors, rows):
    cols = [v.reshape(rows, -1) for v in vectors]
    wide = jnp.concatenate(cols, axis=1)
    return jnp.pad(wide, ((0, 0), (0, 128 - wide.shape[1])))


def body(
    hidden_in,
    row_grad,
    segment_ids,
    query_cls,
    passage_cls,
    positives,
    w_query,
    w_key,
    w_value,
    w_output,
    b_query,
    b_value,
    b_output,
    attn_gain,
    attn_shift,
    w_inner,
    b_inner,
    w_outer,
    b_outer,
    ffn_gain,
    ffn_shift,
    chips,
):
    rows, length, width = hidden_in.shape
    shard = w_query.shape[0]
    cube = Cube(chips)
    inputs = hidden_in.reshape(length, width)
    starts = jnp.stack([query_cls[0], passage_cls[0]], axis=1).reshape(-1)

    vectors = as_columns(
        [b_query, b_value, b_output, attn_gain, attn_shift, b_outer, ffn_gain, ffn_shift, b_inner], shard
    )
    first_shard = jnp.concatenate([w_query, w_key, w_value, vectors], axis=1).astype(BF16)
    hidden = w_inner.shape[1]
    rest_shard = jnp.concatenate([w_output, w_inner, w_outer.reshape(shard, -1)], axis=1).astype(BF16)
    first = cube.gather(first_shard)
    rest = lax.all_gather(rest_shard, AXES, axis=0, tiled=True)
    qkv_mat = first[:, : 3 * width]
    small = first[:, 3 * width :].astype(F32).T
    query_bias, value_bias, output_bias, gain_one, shift_one, outer_bias, gain_two, shift_two = small[:8]
    inner_bias = small[8 : 8 + hidden // width].T.reshape(-1)
    qkv_bias = jnp.concatenate([query_bias, jnp.zeros_like(query_bias), value_bias])
    qkv = (matmul(inputs, qkv_mat) + qkv_bias).astype(BF16)
    context, lse = attn_fwd(starts, qkv)

    output_mat = rest[:, :width]
    inner_mat = rest[:, width : width + hidden]
    outer_mat = rest[:, width + hidden :].reshape(hidden, width)
    branch = matmul(context, output_mat) + output_bias
    middle, normed_one, scaling_one = norm_forward(inputs.astype(F32) + branch, gain_one, shift_one)
    middle_low = middle.astype(BF16)
    pre_act = matmul(middle_low, inner_mat) + inner_bias
    activated, slope = gelu_parts(pre_act)
    act_low = activated.astype(BF16)
    update = matmul(act_low, outer_mat) + outer_bias
    output, normed_two, scaling_two = norm_forward(middle + update, gain_two, shift_two)
    output_low = output.astype(BF16)

    pairs = query_cls.shape[1]
    cls = jnp.concatenate([query_cls[0], passage_cls[0]])
    pick = cls[:, None] == jnp.arange(length, dtype=jnp.int32)[None, :]
    own = matmul(pick.astype(BF16), output_low).astype(BF16)
    everyone = cube.gather(own[None])
    count = everyone.shape[0] * pairs
    all_queries = everyone[:, :pairs].reshape(count, width)
    all_passages = everyone[:, pairs:].reshape(count, width)
    score_scale = 4.0 / math.sqrt(width)
    scores = contract_cols(all_queries, all_passages) * score_scale
    hit = (jnp.arange(count, dtype=jnp.int32)[None, :] == positives[:, None]).astype(F32)
    highest = jnp.max(scores, axis=-1, keepdims=True)
    log_total = highest + jnp.log(jnp.sum(jnp.exp(scores - highest), axis=-1, keepdims=True))
    losses = log_total[:, 0] - jnp.sum(hit * scores, axis=-1)
    score_grad = ((jnp.exp(scores - log_total) - hit) * score_scale).astype(BF16)
    begin = cube.me * pairs
    query_loss = lax.dynamic_slice_in_dim(losses, begin, pairs, 0)
    own_rows = lax.dynamic_slice_in_dim(score_grad, begin, pairs, 0)
    own_cols = lax.dynamic_slice_in_dim(score_grad, begin, pairs, 1)
    cls_grad = jnp.concatenate([matmul(own_rows, all_passages), contract_rows(own_cols, all_queries)])
    added = jnp.einsum("nt,nd->td", pick.astype(F32), cls_grad, precision=lax.Precision.HIGHEST)
    out_grad = row_grad.reshape(length, width).astype(F32) + added

    sum_grad, gain_two_grad, shift_two_grad = norm_backward(out_grad, normed_two, scaling_two, gain_two)
    update_grad = sum_grad.astype(BF16)
    outer_grad = contract_rows(act_low, update_grad).astype(BF16)
    outer_bias_grad = jnp.sum(update_grad.astype(F32), axis=0)
    w_outer_grad = cube.scatter(outer_grad)
    pre_grad = (contract_cols(update_grad, outer_mat) * slope).astype(BF16)
    inner_grad = contract_rows(middle_low, pre_grad).astype(BF16)
    inner_bias_grad = jnp.sum(pre_grad.astype(F32), axis=0)
    w_inner_grad = cube.scatter(inner_grad)
    middle_grad = sum_grad + contract_cols(pre_grad, inner_mat)
    first_grad, gain_one_grad, shift_one_grad = norm_backward(middle_grad, normed_one, scaling_one, gain_one)
    branch_grad = first_grad.astype(BF16)
    output_bias_grad = jnp.sum(branch_grad.astype(F32), axis=0)
    output_w_grad = contract_rows(context, branch_grad).astype(BF16)
    context_grad = contract_cols(branch_grad, output_mat).astype(BF16)

    qkv_grad = attn_bwd(starts, qkv, context_grad, lse)
    qkv_w_grad = contract_rows(inputs, qkv_grad).astype(BF16)
    qkv_bias_grad = jnp.sum(qkv_grad.astype(F32), axis=0)
    hidden_grad = first_grad + contract_cols(qkv_grad, qkv_mat)
    vector_grads = as_columns(
        [
            qkv_bias_grad[:width],
            qkv_bias_grad[2 * width :],
            output_bias_grad,
            gain_one_grad,
            shift_one_grad,
            outer_bias_grad,
            gain_two_grad,
            shift_two_grad,
            inner_bias_grad,
        ],
        width,
    )
    last = cube.scatter(jnp.concatenate([qkv_w_grad, output_w_grad, vector_grads.astype(BF16)], axis=1))
    tail = last[:, 4 * width :]
    vec = [tail[:, j] for j in range(8)]
    return (
        query_loss,
        output_low[None],
        hidden_grad[None],
        last[:, :width],
        last[:, width : 2 * width],
        last[:, 2 * width : 3 * width],
        last[:, 3 * width : 4 * width],
        vec[0],
        vec[1],
        vec[2],
        vec[3],
        vec[4],
        w_inner_grad,
        tail[:, 8 : 8 + hidden // width].reshape(-1),
        w_outer_grad,
        vec[5],
        vec[6],
        vec[7],
    )


def solution(mesh):
    rows3 = P(AXES, None, None)
    rows2 = P(AXES, None)
    rows1 = P(AXES)
    chips = mesh.shape["dp"]

    def run(*args):
        return body(*args, chips=chips)

    return jax.shard_map(
        run,
        mesh=mesh,
        in_specs=(rows3, rows3, rows2, rows2, rows2, P())
        + (rows2,) * 4
        + (rows1,) * 5
        + (rows2, rows1, rows2)
        + (rows1,) * 3,
        out_specs=(rows1, rows3, rows3)
        + (rows2,) * 4
        + (rows1,) * 5
        + (rows2, rows1, rows2)
        + (rows1,) * 3,
        check_vma=False,
    )
```
